128 devices in a mesh: section: 8 (over z_lo, y), dp: 16 (over z_hi, x, core).
Axes of the slice: x: 4, y: 4, z: 4 (z_hi: 2, z_lo: 2; z = z_hi * 2 + z_lo), core: 2. Of those that a mesh axis runs over, the one named last changes fastest.
Arguments:
- enc_in: bfloat16 [8, 2, 8192, 1152], P('section', None, 'dp'), may hold values from -6 to 6
- dec_in: bfloat16 [8, 2, 8192, 1152], P('section', None, 'dp'), may hold values from -6 to 6
- cotangent: bfloat16 [8, 2, 8192, 1152], P('section', None, 'dp'), may hold values from -0.23925781 to 0.23925781
- w_proj: float32 [8, 1152, 1152], P('section', 'dp'), may hold values from -0.1875 to 0.1875
- w_skip: float32 [8, 2304, 1152], P('section', 'dp'), may hold values from -0.125 to 0.125
- m_proj: float32 [8, 1152, 1152], P('section', 'dp'), may hold values from -3 to 3
- v_proj: float32 [8, 1152, 1152], P('section', 'dp'), may hold values from 0.05 to 1
- m_skip: float32 [8, 2304, 1152], P('section', 'dp'), may hold values from -3 to 3
- v_skip: float32 [8, 2304, 1152], P('section', 'dp'), may hold values from 0.05 to 1
Outputs:
- dec_out: bfloat16 [8, 2, 8192, 1152], P('section', None, 'dp')
- enc_grad: bfloat16 [8, 2, 8192, 1152], P('section', None, 'dp')
- dec_grad: bfloat16 [8, 2, 8192, 1152], P('section', None, 'dp')
- new_w_proj: float32 [8, 1152, 1152], P('section', 'dp')
- new_m_proj: float32 [8, 1152, 1152], P('section', 'dp')
- new_v_proj: float32 [8, 1152, 1152], P('section', 'dp')
- new_w_skip: float32 [8, 2304, 1152], P('section', 'dp')
- new_m_skip: float32 [8, 2304, 1152], P('section', 'dp')
- new_v_skip: float32 [8, 2304, 1152], P('section', 'dp')
The draws below stay inside these ranges and needn't reach their ends.
All inputs are finite; a program needn't handle non-finite values.
Results may differ from the reference program's by a relative error of at most 0.025.
Values may be sent and summed in bfloat16 or wider, within the bound.
A program may use at most 128 MiB of HBM per device.

```python
import math
import jax
import jax.numpy as jnp
from jax import lax

D = 1152
MB = 2
TOKENS = 8192
N_SECTION = 8


def level_of(own_key, dims, cuts, least, high):
    factor_of = 1.0
    for position, parts in cuts:
        heights = jax.random.uniform(jax.random.fold_in(jax.random.fold_in(own_key, 6), position), (parts,), jnp.float32, least / len(cuts), high / len(cuts))
        factor_of = factor_of * jnp.repeat(jnp.exp(heights), dims[position] // parts).reshape((-1,) + (1,) * (len(dims) - 1 - position))
    return factor_of


def scatter_about(stream_key, dims, deviation, most, cuts=(), held_as=jnp.bfloat16):
    result = deviation * jax.random.normal(stream_key, dims, jnp.float32)
    if cuts:
        result = result * level_of(stream_key, dims, cuts, -0.22, 0.18)
    return jnp.clip(result, -most, most).astype(held_as)


def setup_inputs(seed: int = 0) -> dict:
    keys = jax.random.split(jax.random.key(seed), 10)
    return {
        "enc_in": scatter_about(keys[0], (N_SECTION, MB, TOKENS, D), 1.0, 6.0, ((0, 8), (2, 16))),
        "dec_in": scatter_about(keys[1], (N_SECTION, MB, TOKENS, D), 1.0, 6.0, ((0, 8), (2, 16))),
        "cotangent": scatter_about(keys[2], (N_SECTION, MB, TOKENS, D), 0.04, 0.23925781, ((0, 8), (2, 16))),
        "w_proj": scatter_about(keys[3], (N_SECTION, D, D), D ** -0.5, 0.1875, ((0, 8), (1, 16)), jnp.float32),
        "w_skip": scatter_about(keys[4], (N_SECTION, 2 * D, D), (2 * D) ** -0.5, 0.125, ((0, 8), (1, 16)), jnp.float32),
        "m_proj": scatter_about(keys[5], (N_SECTION, D, D), 0.5, 3.0, ((0, 8), (1, 16)), jnp.float32),
        "v_proj": jnp.clip(jnp.exp(math.log(1.0) - 2.9957323 * jax.random.uniform(keys[6], (N_SECTION, D, D), jnp.float32) ** level_of(keys[6], (N_SECTION, D, D), ((0, 8), (1, 16)), -0.2, 0.2)), 0.05, 1.0),
        "m_skip": scatter_about(keys[7], (N_SECTION, 2 * D, D), 0.5, 3.0, ((0, 8), (1, 16)), jnp.float32),
        "v_skip": jnp.clip(jnp.exp(math.log(1.0) - 2.9957323 * jax.random.uniform(keys[8], (N_SECTION, 2 * D, D), jnp.float32) ** level_of(keys[8], (N_SECTION, 2 * D, D), ((0, 8), (1, 16)), -0.2, 0.2)), 0.05, 1.0),
    }


half_root = 0.7071067811865476
gauss_norm = 0.3989422804014327
beta_one = 0.9
beta_two = 0.95
learn_rate = 0.002
adam_eps = 1e-08
correct_one = 1.0 - 0.9 ** 10
correct_two = 1.0 - 0.95 ** 10

def gelu_parts(preact):
    normal_cdf = 0.5 * (1.0 + lax.erf(preact * half_root))
    density = jnp.exp(-0.5 * preact * preact) * gauss_norm
    return (preact * normal_cdf, normal_cdf + preact * density)

def adam_update(weight, moment, second, grad):
    new_moment = beta_one * moment + (1.0 - beta_one) * grad
    new_second = beta_two * second + (1.0 - beta_two) * grad * grad
    step_size = new_moment / correct_one / (jnp.sqrt(new_second / correct_two) + adam_eps)
    return (weight - learn_rate * step_size, new_moment, new_second)

def partner_of(section):
    return (section + N_SECTION // 2) % N_SECTION

def reference(enc_in, dec_in, cotangent, w_proj, w_skip, m_proj, v_proj, m_skip, v_skip):
    rows = MB * TOKENS
    proj_half = w_proj.astype(jnp.bfloat16)
    skip_half = w_skip.astype(jnp.bfloat16)
    skips = []
    for section in range(N_SECTION):
        enc_rows = enc_in[section].reshape(rows, D)
        skips.append(jnp.dot(enc_rows, proj_half[section], preferred_element_type=jnp.float32).astype(jnp.bfloat16))
    dec_outs = []
    dec_grads = []
    grad_skips = []
    skip_grads = [None] * N_SECTION
    for section in range(N_SECTION):
        dec_rows = dec_in[section].reshape(rows, D)
        joined = jnp.concatenate([dec_rows, skips[partner_of(section)]], axis=1)
        preact = jnp.dot(joined, skip_half[section], preferred_element_type=jnp.float32)
        activated, gelu_slope = gelu_parts(preact)
        dec_outs.append(activated.astype(jnp.bfloat16).reshape(MB, TOKENS, D))
        out_grad = cotangent[section].reshape(rows, D).astype(jnp.float32)
        pre_grad = (out_grad * gelu_slope).astype(jnp.bfloat16)
        input_grad = jnp.dot(pre_grad, skip_half[section].T, preferred_element_type=jnp.float32)
        dec_grads.append(input_grad[:, :D].astype(jnp.bfloat16).reshape(MB, TOKENS, D))
        skip_grads[partner_of(section)] = input_grad[:, D:].astype(jnp.bfloat16)
        grad_skips.append(jnp.dot(joined.T, pre_grad, preferred_element_type=jnp.float32))
    enc_grads = []
    grad_projs = []
    for section in range(N_SECTION):
        enc_rows = enc_in[section].reshape(rows, D)
        enc_grads.append(jnp.dot(skip_grads[section], proj_half[section].T, preferred_element_type=jnp.float32).astype(jnp.bfloat16).reshape(MB, TOKENS, D))
        grad_projs.append(jnp.dot(enc_rows.T, skip_grads[section], preferred_element_type=jnp.float32))
    new_w_proj, new_m_proj, new_v_proj = adam_update(w_proj, m_proj, v_proj, jnp.stack(grad_projs, 0))
    new_w_skip, new_m_skip, new_v_skip = adam_update(w_skip, m_skip, v_skip, jnp.stack(grad_skips, 0))
    return (jnp.stack(dec_outs, 0), jnp.stack(enc_grads, 0), jnp.stack(dec_grads, 0), new_w_proj, new_m_proj, new_v_proj, new_w_skip, new_m_skip, new_v_skip)
```

```python
import jax
import jax.numpy as jnp
from jax import lax
from jax.sharding import PartitionSpec as P

half_root = 0.7071067811865476
gauss_norm = 0.3989422804014327
beta_one = 0.9
beta_two = 0.95
learn_rate = 0.002
adam_eps = 1e-08
correct_one = 1.0 - 0.9**10
correct_two = 1.0 - 0.95**10


def swapped(value, axis, bit):
    mask = 2**bit
    pairs = [(source, source ^ mask) for source in range(lax.axis_size(axis))]
    return lax.ppermute(value, axis, pairs)


def gelu_parts(preact):
    normal_cdf = 0.5 * (1.0 + lax.erf(preact * half_root))
    density = jnp.exp(-0.5 * preact * preact) * gauss_norm
    return (preact * normal_cdf, normal_cdf + preact * density)


def adam_update(weight, moment, second, grad):
    new_moment = beta_one * moment + (1.0 - beta_one) * grad
    new_second = beta_two * second + (1.0 - beta_two) * grad * grad
    step_size = new_moment / correct_one / (jnp.sqrt(new_second / correct_two) + adam_eps)
    return (weight - learn_rate * step_size, new_moment, new_second)


def swap_partner(value):
    bit = lax.axis_size("section").bit_length() - 2
    return swapped(value, "section", bit)


def body(enc_in, dec_in, cotangent, w_proj, w_skip, m_proj, v_proj, m_skip, v_skip):
    micro, tokens_here, width = enc_in.shape[1:]
    rows = micro * tokens_here
    enc_rows = swap_partner(enc_in[0].reshape(rows, width))
    proj_shard = swap_partner(w_proj[0].astype(jnp.bfloat16))
    proj_full = lax.all_gather(proj_shard, "dp", axis=0, tiled=True)
    skip_full = lax.all_gather(w_skip[0].astype(jnp.bfloat16), "dp", axis=0, tiled=True)
    dec_rows = dec_in[0].reshape(rows, width)
    out_grad = cotangent[0].reshape(rows, width)
    skip = jnp.dot(enc_rows, proj_full, preferred_element_type=jnp.float32).astype(jnp.bfloat16)
    preact = jnp.dot(dec_rows, skip_full[:width], preferred_element_type=jnp.float32) + jnp.dot(
        skip, skip_full[width:], preferred_element_type=jnp.float32
    )
    activated, gelu_slope = gelu_parts(preact)
    dec_out = activated.astype(jnp.bfloat16)
    pre_grad = (out_grad.astype(jnp.float32) * gelu_slope).astype(jnp.bfloat16)
    skip_grad = jnp.einsum(
        "rk,jk->rj", pre_grad, skip_full[width:], preferred_element_type=jnp.float32
    ).astype(jnp.bfloat16)
    enc_grad = swap_partner(
        jnp.einsum("rk,jk->rj", skip_grad, proj_full, preferred_element_type=jnp.float32).astype(
            jnp.bfloat16
        )
    )
    dec_grad = jnp.einsum(
        "rk,jk->rj", pre_grad, skip_full[:width], preferred_element_type=jnp.float32
    ).astype(jnp.bfloat16)
    grad_dec = jnp.einsum("rj,rk->jk", dec_rows, pre_grad, preferred_element_type=jnp.float32)
    grad_mid = jnp.einsum("rj,rk->jk", skip, pre_grad, preferred_element_type=jnp.float32)
    grad_skip = jnp.concatenate([grad_dec, grad_mid], axis=0).astype(jnp.bfloat16)
    grad_proj = jnp.einsum(
        "rj,rk->jk", enc_rows, skip_grad, preferred_element_type=jnp.float32
    ).astype(jnp.bfloat16)
    count = lax.axis_size("dp")
    grads = jnp.concatenate(
        [
            grad_skip.reshape(count, -1, width),
            jnp.pad(grad_proj.reshape(count, -1, width), ((0, 0), (0, 8), (0, 0))),
        ],
        axis=1,
    )
    shard = lax.psum_scatter(grads, "dp", scatter_dimension=0, tiled=True)[0]
    proj_sum = swap_partner(shard[w_skip.shape[1] :][: w_proj.shape[1]])
    skip_sum = shard[: w_skip.shape[1]]
    new_w_proj, new_m_proj, new_v_proj = adam_update(
        w_proj[0], m_proj[0], v_proj[0], proj_sum.astype(jnp.float32)
    )
    new_w_skip, new_m_skip, new_v_skip = adam_update(
        w_skip[0], m_skip[0], v_skip[0], skip_sum.astype(jnp.float32)
    )
    shape = (1, micro, tokens_here, width)
    return (
        dec_out.reshape(shape),
        enc_grad.reshape(shape),
        dec_grad.reshape(shape),
        new_w_proj[None],
        new_m_proj[None],
        new_v_proj[None],
        new_w_skip[None],
        new_m_skip[None],
        new_v_skip[None],
    )


def solution(mesh):
    in_specs = (
        P("section", None, "dp", None),
        P("section", None, "dp", None),
        P("section", None, "dp", None),
        P("section", "dp", None),
        P("section", "dp", None),
        P("section", "dp", None),
        P("section", "dp", None),
        P("section", "dp", None),
        P("section", "dp", None),
    )
    out_specs = (
        P("section", None, "dp", None),
        P("section", None, "dp", None),
        P("section", None, "dp", None),
        P("section", "dp", None),
        P("section", "dp", None),
        P("section", "dp", None),
        P("section", "dp", None),
        P("section", "dp", None),
        P("section", "dp", None),
    )
    return jax.shard_map(body, mesh=mesh, in_specs=in_specs, out_specs=out_specs, check_vma=False)
```
